32 devices in a mesh: chan: 4 (over z), ctx: 8 (over y, x, core).
Axes of the slice: x: 2, y: 2, z: 4, core: 2. Of those that a mesh axis runs over, the one named last changes fastest.
Arguments:
- queries: bfloat16 [8192, 1024], P('chan', 'ctx'), may hold values from -6 to 6
- keys: bfloat16 [8192, 1024], P('chan', 'ctx'), may hold values from -6 to 6
- values: bfloat16 [8192, 1024], P('chan', 'ctx'), may hold values from -6 to 6
- out_grad: bfloat16 [1024, 8192], P('ctx', 'chan'), may hold values from -6 to 6
- out_weight: bfloat16 [8192, 8192], P('chan'), may hold values from -0.0625 to 0.0625
- residues: float32 [16, 8192], P(None, 'chan'), may hold values from -1.5 to 1.5
- decay_rates: float32 [16, 8192], P(None, 'chan'), may hold values from 0.00048828125 to 1
Outputs:
- query_grad: bfloat16 [8192, 1024], P('chan', 'ctx')
- key_grad: bfloat16 [8192, 1024], P('chan', 'ctx')
- value_grad: bfloat16 [8192, 1024], P('chan', 'ctx')
- resid_grad: float32 [16, 8192], P(None, ('chan', 'ctx'))
- decay_grad: float32 [16, 8192], P(None, ('chan', 'ctx'))
The draws below stay inside these ranges and needn't reach their ends.
All inputs are finite; a program needn't handle non-finite values.
Results may differ from the reference program's by a relative error of at most 0.0085.
Values may be sent and summed in bfloat16 or wider, within the bound.
A program may use at most 192 MiB of HBM per device.

```python
import math
import jax
import jax.numpy as jnp
from jax import lax

D = 8192
ORDER = 16
B = 1024
SEQ = 1024


def draw_queries(key, part):
    own_key = jax.random.fold_in(key, 101)
    gate_values = jnp.clip(jax.random.normal(jax.random.fold_in(own_key, 1), (D, SEQ), jnp.float32), -6.0, 6.0)
    return gate_values.astype(jnp.bfloat16)


def draw_keys(key, part):
    own_key = jax.random.fold_in(key, 102)
    gate_values = jnp.clip(jax.random.normal(jax.random.fold_in(own_key, 1), (D, SEQ), jnp.float32), -6.0, 6.0)
    return gate_values.astype(jnp.bfloat16)


def draw_values(key, part):
    own_key = jax.random.fold_in(key, 103)
    white_noise = jax.random.normal(jax.random.fold_in(own_key, 1), (D, SEQ), jnp.float32)
    return jnp.clip(white_noise, -6.0, 6.0).astype(jnp.bfloat16)


def draw_out_grad(key, part):
    own_key = jax.random.fold_in(key, 104)
    white_noise = jax.random.normal(jax.random.fold_in(own_key, 1), (SEQ, D), jnp.float32)
    return jnp.clip(white_noise, -6.0, 6.0).astype(jnp.bfloat16)


def filter_modes(key):
    mode_key = jax.random.fold_in(key, 105)
    spread = jax.random.uniform(jax.random.fold_in(mode_key, 1), (ORDER, D), jnp.float32)
    magnitude = jax.random.uniform(jax.random.fold_in(mode_key, 2), (ORDER, D), jnp.float32)
    coin_flips = jax.random.randint(jax.random.fold_in(mode_key, 3), (ORDER, D), 0, 2)
    sign_values = (1 - 2 * coin_flips).astype(jnp.float32)
    balance = jax.random.uniform(jax.random.fold_in(mode_key, 5), (ORDER, D), jnp.float32, 0.95, 1.0)
    slow_count = max(1, ORDER // 8)
    fast_count = ORDER // 4
    pair_count = (ORDER - slow_count - fast_count) // 2
    rate_rows = []
    resid_rows = []
    for slot_index in range(slow_count):
        rate_rows.append(jnp.exp(math.log(0.5) + spread[slot_index] * math.log(8.0)) / SEQ)
        resid_rows.append(sign_values[slot_index] * (0.2 + 0.4 * magnitude[slot_index]))
    for pair_index in range(pair_count):
        first_slot = slow_count + 2 * pair_index
        base_rate = jnp.exp(math.log(40.0) + spread[first_slot] * math.log(2.5)) / SEQ
        leading = jnp.minimum(base_rate, 1.0)
        trailing = jnp.minimum(0.5 * base_rate, 1.0)
        lead_resid = sign_values[first_slot] * (0.5 + 0.5 * magnitude[first_slot])
        rate_rows.append(leading)
        rate_rows.append(trailing)
        resid_rows.append(lead_resid)
        resid_rows.append(-lead_resid * jnp.sqrt(leading / trailing) * balance[first_slot])
    for slot_index in range(slow_count + 2 * pair_count, ORDER):
        rate_rows.append(jnp.minimum(jnp.exp(math.log(200.0) + spread[slot_index] * math.log(10.0)) / SEQ, 1.0))
        resid_rows.append(sign_values[slot_index] * (0.08 + 0.12 * magnitude[slot_index]))
    role_rates = jnp.stack(rate_rows)
    role_resid = jnp.stack(resid_rows)
    scores = jax.random.randint(jax.random.fold_in(mode_key, 4), (ORDER, D), 0, 1 << 20) * ORDER + jnp.arange(ORDER, dtype=jnp.int32)[:, None]
    order_index = jnp.argsort(scores, axis=0)
    return (jnp.take_along_axis(role_rates, order_index, axis=0), jnp.take_along_axis(role_resid, order_index, axis=0))


def draw_residues(key, part):
    mode_rates, mode_resid = filter_modes(key)
    return mode_resid.astype(jnp.float32)


def draw_decay_rates(key, part):
    mode_rates, mode_resid = filter_modes(key)
    return mode_rates.astype(jnp.float32)


def block_levels(key, extent, cuts, smallest, largest):
    level = 1.0
    for position, parts in cuts:
        steps = jax.random.uniform(jax.random.fold_in(jax.random.fold_in(key, 6), position), (parts,), jnp.float32, smallest / len(cuts), largest / len(cuts))
        level = level * jnp.repeat(jnp.exp(steps), extent[position] // parts).reshape((-1,) + (1,) * (len(extent) - 1 - position))
    return level


def noise(key, shape, scale, reach, shards=(), kind=jnp.bfloat16):
    loudness = block_levels(key, shape, shards, -0.22, 0.18) if shards else 1.0
    entries = jax.random.normal(key, shape, jnp.float32) * scale * loudness
    return jnp.minimum(jnp.maximum(entries, -reach), reach).astype(kind)


def setup_inputs(seed: int = 0) -> dict:
    seeds = jax.random.split(jax.random.key(seed), 8)
    return {
        "queries": draw_queries(jax.random.fold_in(seeds[7], 71), 0),
        "keys": draw_keys(jax.random.fold_in(seeds[7], 71), 0),
        "values": draw_values(jax.random.fold_in(seeds[7], 71), 0),
        "out_grad": draw_out_grad(jax.random.fold_in(seeds[7], 71), 0),
        "out_weight": noise(seeds[4], (D, D), D ** -0.5, 0.0625, ((0, 4),)),
        "residues": draw_residues(jax.random.fold_in(seeds[7], 71), 0),
        "decay_rates": draw_decay_rates(jax.random.fold_in(seeds[7], 71), 0),
    }


PRECISE = lax.Precision.HIGHEST

def dft_tables(block_size, section_size):
    total_size = section_size * block_size
    inner = jnp.arange(block_size, dtype=jnp.int32)
    outer = jnp.arange(section_size, dtype=jnp.int32)
    half_size = section_size // 2
    inner_angle = (inner[:, None] * inner[None, :] % block_size).astype(jnp.float32) * (2.0 * math.pi / block_size)
    twist_angle = (outer[:, None] * inner[None, :] % total_size).astype(jnp.float32) * (2.0 * math.pi / total_size)
    outer_rows = jnp.arange(half_size, dtype=jnp.int32)
    outer_angle = (outer_rows[:, None] * outer[None, :] % section_size).astype(jnp.float32) * (2.0 * math.pi / section_size)
    return (jnp.cos(inner_angle).astype(jnp.bfloat16), jnp.sin(inner_angle).astype(jnp.bfloat16), jnp.cos(twist_angle), jnp.sin(twist_angle), jnp.cos(outer_angle).astype(jnp.bfloat16), jnp.sin(outer_angle).astype(jnp.bfloat16))

def forward(signal, tables):
    big_cos, big_sin, twist_cos, twist_sin, small_cos, small_sin = tables
    channels = signal.shape[0]
    half_size, section_size = small_cos.shape
    block_size = big_cos.shape[0]
    grid_view = signal.astype(jnp.float32).reshape(channels, half_size, block_size)
    outer_cos = small_cos.astype(jnp.float32)
    outer_sin = small_sin.astype(jnp.float32)
    real_part = jnp.einsum('chb,hk->ckb', grid_view, outer_cos, precision=PRECISE)
    imag_part = -jnp.einsum('chb,hk->ckb', grid_view, outer_sin, precision=PRECISE)
    turned_re = (real_part * twist_cos + imag_part * twist_sin).astype(jnp.bfloat16).reshape(channels * section_size, block_size)
    turned_im = (imag_part * twist_cos - real_part * twist_sin).astype(jnp.bfloat16).reshape(channels * section_size, block_size)
    out_re = jnp.dot(turned_re, big_cos, preferred_element_type=jnp.float32) + jnp.dot(turned_im, big_sin, preferred_element_type=jnp.float32)
    out_im = jnp.dot(turned_im, big_cos, preferred_element_type=jnp.float32) - jnp.dot(turned_re, big_sin, preferred_element_type=jnp.float32)
    return (out_re.reshape(channels, section_size, block_size), out_im.reshape(channels, section_size, block_size))

def inverse(spec_re, spec_im, tables):
    big_cos, big_sin, twist_cos, twist_sin, small_cos, small_sin = tables
    channels, section_size, block_size = spec_re.shape
    half_size = small_cos.shape[0]
    flat_re = spec_re.astype(jnp.bfloat16).reshape(channels * section_size, block_size)
    flat_im = spec_im.astype(jnp.bfloat16).reshape(channels * section_size, block_size)
    back_re = jnp.dot(flat_re, big_cos, preferred_element_type=jnp.float32) - jnp.dot(flat_im, big_sin, preferred_element_type=jnp.float32)
    back_im = jnp.dot(flat_re, big_sin, preferred_element_type=jnp.float32) + jnp.dot(flat_im, big_cos, preferred_element_type=jnp.float32)
    back_re = back_re.reshape(channels, section_size, block_size)
    back_im = back_im.reshape(channels, section_size, block_size)
    wound_re = lax.optimization_barrier((back_re * twist_cos - back_im * twist_sin).astype(jnp.bfloat16)).astype(jnp.float32)
    wound_im = lax.optimization_barrier((back_re * twist_sin + back_im * twist_cos).astype(jnp.bfloat16)).astype(jnp.float32)
    outer_cos = small_cos.astype(jnp.float32)
    outer_sin = small_sin.astype(jnp.float32)
    grid_view = jnp.einsum('ckb,hk->chb', wound_re, outer_cos, precision=PRECISE) - jnp.einsum('ckb,hk->chb', wound_im, outer_sin, precision=PRECISE)
    return grid_view.reshape(channels, half_size * block_size) * (1.0 / (section_size * block_size))

def filter_spectrum(resid, rates, tables):
    small_cos = tables[4]
    section_size = small_cos.shape[1]
    block_size = tables[0].shape[0]
    total_size = section_size * block_size
    seq_length = total_size // 2
    frequency = jnp.arange(section_size, dtype=jnp.int32)[:, None] + section_size * jnp.arange(block_size, dtype=jnp.int32)[None, :]
    half_angle = frequency.astype(jnp.float32) * (math.pi / total_size)
    sine_half = jnp.sin(half_angle)
    sine_square = sine_half * sine_half
    sine_full = jnp.sin(2.0 * half_angle)
    parity = 1.0 - 2.0 * (frequency % 2).astype(jnp.float32)

    def add_mode(running, mode_vals):
        decay_rate, amplitude = mode_vals
        ratio = jnp.exp(-decay_rate)[:, None, None]
        one_minus = (-jnp.expm1(-decay_rate))[:, None, None]
        tail_value = jnp.exp(-decay_rate * seq_length)[:, None, None]
        root_gain = (amplitude * jnp.sqrt(2.0 * decay_rate))[:, None, None]
        den_real = one_minus + 2.0 * ratio * sine_square
        den_imag = ratio * sine_full
        modulus = one_minus * one_minus + 4.0 * ratio * sine_square
        numerator = root_gain * (1.0 - tail_value * parity) / modulus
        return ((running[0] + numerator * den_real, running[1] - numerator * den_imag), None)
    channels = resid.shape[1]
    initial = (jnp.zeros((channels, section_size, block_size), jnp.float32), jnp.zeros((channels, section_size, block_size), jnp.float32))
    result, unused = lax.scan(add_mode, initial, (rates, resid))
    return result

def filter_grads(kernel_grad, resid, rates):
    positions = jnp.arange(kernel_grad.shape[1], dtype=jnp.int32).astype(jnp.float32)

    def one_mode(unused_carry, mode_vals):
        decay_rate, amplitude = mode_vals
        decay_curve = jnp.exp(-decay_rate[:, None] * positions[None, :])
        weighted = kernel_grad * decay_curve
        plain_sum = lax.optimization_barrier(jnp.sum(weighted, axis=1))
        moment_sum = lax.optimization_barrier(jnp.sum(weighted * positions[None, :], axis=1))
        root_gain = jnp.sqrt(2.0 * decay_rate)
        return (unused_carry, (root_gain * plain_sum, amplitude * root_gain * (0.5 * plain_sum - decay_rate * moment_sum)))
    unused, grads = lax.scan(one_mode, jnp.zeros((), jnp.float32), (rates, resid))
    return grads

def conv_core(product, conv_grad, resid, rates, tables):
    spec_re, spec_im = filter_spectrum(resid, rates, tables)
    src_re, src_im = forward(product, tables)
    drv_re, drv_im = forward(conv_grad, tables)
    conv_out = inverse(spec_re * src_re - spec_im * src_im, spec_re * src_im + spec_im * src_re, tables).astype(jnp.bfloat16)
    product_grad = inverse(spec_re * drv_re + spec_im * drv_im, spec_re * drv_im - spec_im * drv_re, tables).astype(jnp.bfloat16)
    kernel_grad = inverse(drv_re * src_re + drv_im * src_im, drv_im * src_re - drv_re * src_im, tables)
    resid_grad, decay_grad = filter_grads(kernel_grad, resid, rates)
    return (conv_out, product_grad, resid_grad, decay_grad)

def reference(queries, keys, values, out_grad, out_weight, residues, decay_rates):
    channels, seq_length = queries.shape
    section_size = 2 * seq_length // B
    tables = dft_tables(B, section_size)
    mixer_grad = jnp.dot(out_weight, out_grad.T, preferred_element_type=jnp.float32).astype(jnp.bfloat16)
    group_width = 64
    block_count = channels // group_width

    def one_block(block_index):
        first_row = block_index * group_width
        query_rows = lax.dynamic_slice_in_dim(queries, first_row, group_width, 0)
        key_rows = lax.dynamic_slice_in_dim(keys, first_row, group_width, 0)
        value_rows = lax.dynamic_slice_in_dim(values, first_row, group_width, 0)
        mixer_rows = lax.dynamic_slice_in_dim(mixer_grad, first_row, group_width, 0)
        resid = lax.dynamic_slice_in_dim(residues, first_row, group_width, 1)
        rates = lax.dynamic_slice_in_dim(decay_rates, first_row, group_width, 1)
        product = (key_rows.astype(jnp.float32) * value_rows.astype(jnp.float32)).astype(jnp.bfloat16)
        conv_grad = (mixer_rows.astype(jnp.float32) * query_rows.astype(jnp.float32)).astype(jnp.bfloat16)
        conv_out, product_grad, resid_grad, decay_grad = conv_core(product, conv_grad, resid, rates, tables)
        query_grad = (mixer_rows.astype(jnp.float32) * conv_out.astype(jnp.float32)).astype(jnp.bfloat16)
        key_grad = (product_grad.astype(jnp.float32) * value_rows.astype(jnp.float32)).astype(jnp.bfloat16)
        value_grad = (product_grad.astype(jnp.float32) * key_rows.astype(jnp.float32)).astype(jnp.bfloat16)
        return (query_grad, key_grad, value_grad, resid_grad, decay_grad)
    query_grad, key_grad, value_grad, resid_grad, decay_grad = lax.map(one_block, jnp.arange(block_count, dtype=jnp.int32))
    order_count = residues.shape[0]
    return (query_grad.reshape(channels, seq_length), key_grad.reshape(channels, seq_length), value_grad.reshape(channels, seq_length), jnp.transpose(resid_grad, (1, 0, 2)).reshape(order_count, channels), jnp.transpose(decay_grad, (1, 0, 2)).reshape(order_count, channels))
```

```python
import functools

import jax
import jax.numpy as jnp
from jax import lax
from jax.experimental import pallas as pl
from jax.experimental.pallas import tpu as pltpu
from jax.sharding import PartitionSpec as P

STEP = 16


def halves(width):
    lanes = min(width, 128)
    return [(start, lanes) for start in range(0, width, lanes)]


def fold_rows(rows):
    lanes = rows[0].shape[1]
    sub = lax.broadcasted_iota(jnp.int32, (8, lanes), 0)
    low4, low2, low1 = sub < 4, (sub & 2) == 0, (sub & 1) == 0
    four = []
    for i in range(4):
        a, b = rows[i], rows[i + 4]
        four.append(jnp.where(low4, a, b) + pltpu.roll(jnp.where(low4, b, a), 4, 0))
    two = []
    for i in range(2):
        a, b = four[i], four[i + 2]
        two.append(
            jnp.where(low2, a, pltpu.roll(b, 2, 0)) + jnp.where(low2, pltpu.roll(a, 6, 0), b)
        )
    a, b = two
    return jnp.where(low1, a, pltpu.roll(b, 1, 0)) + jnp.where(low1, pltpu.roll(a, 7, 0), b)


def mode_groups(rates_ref, resid_ref, start, lanes):
    groups = []
    for first in range(0, rates_ref.shape[0], 8):
        rate = rates_ref[pl.ds(first, 8), pl.ds(start, lanes)]
        gain = resid_ref[pl.ds(first, 8), pl.ds(start, lanes)] * jnp.sqrt(2.0 * rate)
        groups.append((jnp.exp(-rate), gain))
    return groups


def causal_scan(rates_ref, resid_ref, source_ref, out_ref):
    tokens, width = source_ref.shape
    columns = halves(width)
    modes = [mode_groups(rates_ref, resid_ref, *column) for column in columns]
    count = len(modes[0])

    def block(index, state):
        base = pl.multiple_of(index * STEP, STEP)
        state = [list(group) for group in state]
        for position, (start, lanes) in enumerate(columns):
            rows = source_ref[pl.ds(base, STEP), pl.ds(start, lanes)].astype(jnp.float32)
            sums = []
            for step in range(STEP):
                row = jnp.broadcast_to(rows[step : step + 1, :], (8, lanes))
                total = None
                for g in range(count):
                    decay, gain = modes[position][g]
                    held = decay * state[position][g] + row
                    state[position][g] = held
                    total = gain * held if total is None else total + gain * held
                sums.append(total)
            out_ref[pl.ds(base, STEP), pl.ds(start, lanes)] = jnp.concatenate(
                [fold_rows(sums[:8]), fold_rows(sums[8:])], axis=0
            ).astype(out_ref.dtype)
        return tuple(tuple(group) for group in state)

    zero = tuple(
        tuple(jnp.zeros((8, lanes), jnp.float32) for _ in range(count)) for _, lanes in columns
    )
    lax.fori_loop(0, tokens // STEP, block, zero)


def reverse_scan(
    rates_ref, resid_ref, source_ref, drive_ref, out_ref, resid_grad_ref, decay_grad_ref
):
    tokens, width = source_ref.shape
    columns = halves(width)
    modes = [mode_groups(rates_ref, resid_ref, *column) for column in columns]
    count = len(modes[0])
    blocks = tokens // STEP

    def block(index, state):
        base = pl.multiple_of((blocks - 1 - index) * STEP, STEP)
        state = [[list(item) for item in group] for group in state]
        for position, (start, lanes) in enumerate(columns):
            where = (pl.ds(base, STEP), pl.ds(start, lanes))
            source = source_ref[where].astype(jnp.float32)
            drive = drive_ref[where].astype(jnp.float32)
            sums = [None] * STEP
            for step in reversed(range(STEP)):
                source_row = jnp.broadcast_to(source[step : step + 1, :], (8, lanes))
                drive_row = jnp.broadcast_to(drive[step : step + 1, :], (8, lanes))
                total = None
                for g in range(count):
                    decay, gain = modes[position][g]
                    held, moment, plain_sum, moment_sum = state[position][g]
                    moment = decay * (moment + held)
                    held = decay * held + drive_row
                    state[position][g] = [
                        held,
                        moment,
                        plain_sum + source_row * held,
                        moment_sum + source_row * moment,
                    ]
                    total = gain * held if total is None else total + gain * held
                sums[step] = total
            out_ref[where] = jnp.concatenate(
                [fold_rows(sums[:8]), fold_rows(sums[8:])], axis=0
            ).astype(out_ref.dtype)
        return tuple(tuple(tuple(item) for item in group) for group in state)

    zero = tuple(
        tuple((jnp.zeros((8, lanes), jnp.float32),) * 4 for _ in range(count))
        for _, lanes in columns
    )
    final = lax.fori_loop(0, blocks, block, zero)
    for position, (start, lanes) in enumerate(columns):
        for g in range(count):
            where = (pl.ds(8 * g, 8), pl.ds(start, lanes))
            rate, amplitude = rates_ref[where], resid_ref[where]
            root = jnp.sqrt(2.0 * rate)
            plain_sum, moment_sum = final[position][g][2:]
            resid_grad_ref[where] = root * plain_sum
            decay_grad_ref[where] = amplitude * root * (0.5 * plain_sum - rate * moment_sum)


def elementwise(left, right):
    return (left.astype(jnp.float32) * right.astype(jnp.float32)).astype(jnp.bfloat16)


def local(queries, keys, values, out_grad, out_weight, residues, decay_rates):
    channels, tokens = queries.shape
    ctx_size = lax.axis_size("ctx")
    width = channels // ctx_size
    seq_length = tokens * ctx_size
    order = residues.shape[0]
    offset = lax.axis_index("ctx") * width
    resid = lax.dynamic_slice_in_dim(residues, offset, width, 1)
    rates = lax.dynamic_slice_in_dim(decay_rates, offset, width, 1)
    gathered = lax.all_gather(out_grad, "chan", axis=1, tiled=True)
    product = lax.all_to_all(
        elementwise(keys, values).T, "ctx", split_axis=1, concat_axis=0, tiled=True
    )
    sequence = jax.ShapeDtypeStruct((seq_length, width), jnp.bfloat16)
    grads = jax.ShapeDtypeStruct((order, width), jnp.float32)
    cost = pl.CostEstimate(
        flops=10 * order * seq_length * width, bytes_accessed=4 * seq_length * width, transcendentals=0
    )
    conv_out = pl.pallas_call(causal_scan, out_shape=sequence, cost_estimate=cost)(
        rates, resid, product
    )
    conv_out = lax.all_to_all(conv_out, "ctx", split_axis=0, concat_axis=1, tiled=True)
    mixer_grad = jnp.einsum(
        "cd,td->ct", out_weight, gathered, preferred_element_type=jnp.float32
    ).astype(jnp.bfloat16)
    conv_grad = lax.all_to_all(
        elementwise(mixer_grad, queries).T, "ctx", split_axis=1, concat_axis=0, tiled=True
    )
    product_grad, resid_grad, decay_grad = pl.pallas_call(
        reverse_scan, out_shape=(sequence, grads, grads), cost_estimate=cost
    )(rates, resid, product, conv_grad)
    product_grad = lax.all_to_all(product_grad, "ctx", split_axis=0, concat_axis=1, tiled=True).T
    return (
        elementwise(mixer_grad, conv_out.T),
        elementwise(product_grad, values),
        elementwise(product_grad, keys),
        resid_grad,
        decay_grad,
    )


def solution(mesh):
    placed = (
        P("chan", "ctx"),
        P("chan", "ctx"),
        P("chan", "ctx"),
        P("ctx", "chan"),
        P("chan", None),
        P(None, "chan"),
        P(None, "chan"),
    )
    return jax.shard_map(
        local,
        mesh=mesh,
        in_specs=placed,
        out_specs=(
            P("chan", "ctx"),
            P("chan", "ctx"),
            P("chan", "ctx"),
            P(None, ("chan", "ctx")),
            P(None, ("chan", "ctx")),
        ),
        check_vma=False,
    )
```

```python
import functools

import jax
import jax.numpy as jnp
from jax import lax
from jax.experimental import pallas as pl
from jax.experimental.pallas import tpu as pltpu
from jax.sharding import PartitionSpec as P

STEP = 16


def halves(width):
    lanes = min(width, 128)
    return [(start, lanes) for start in range(0, width, lanes)]


def fold_rows(rows):
    lanes = rows[0].shape[1]
    sub = lax.broadcasted_iota(jnp.int32, (8, lanes), 0)
    low4, low2, low1 = sub < 4, (sub & 2) == 0, (sub & 1) == 0
    four = []
    for i in range(4):
        a, b = rows[i], rows[i + 4]
        four.append(jnp.where(low4, a, b) + pltpu.roll(jnp.where(low4, b, a), 4, 0))
    two = []
    for i in range(2):
        a, b = four[i], four[i + 2]
        two.append(
            jnp.where(low2, a, pltpu.roll(b, 2, 0)) + jnp.where(low2, pltpu.roll(a, 6, 0), b)
        )
    a, b = two
    return jnp.where(low1, a, pltpu.roll(b, 1, 0)) + jnp.where(low1, pltpu.roll(a, 7, 0), b)


def axis_device(axis, index):
    return {axis: index}


def exchange(outgoing, incoming, sends, arrivals, me, other):
    return pltpu.make_async_remote_copy(
        src_ref=outgoing.at[other],
        dst_ref=incoming.at[me],
        send_sem=sends.at[other],
        recv_sem=arrivals.at[me],
        device_id=axis_device("ctx", other),
        device_id_type=pl.DeviceIdType.MESH,
    )


def expect(outgoing, incoming, sends, arrivals, other):
    return pltpu.make_async_remote_copy(
        src_ref=outgoing.at[other],
        dst_ref=incoming.at[other],
        send_sem=sends.at[other],
        recv_sem=arrivals.at[other],
        device_id=axis_device("ctx", other),
        device_id_type=pl.DeviceIdType.MESH,
    )


def body(
    chan_size,
    ctx_size,
    queries,
    keys,
    values,
    out_grad,
    out_weight,
    residues,
    decay_rates,
    query_grad,
    key_grad,
    value_grad,
    resid_grad,
    decay_grad,
    weight,
    gathered,
    mixer,
    product_out,
    product_in,
    conv_out_out,
    conv_out_in,
    conv_grad_out,
    conv_grad_in,
    product_grad_out,
    product_grad_in,
    weight_sems,
    shard_arrivals,
    up_sends,
    down_sends,
    sends,
    arrivals,
):
    place = lax.axis_index("chan")
    me = lax.axis_index("ctx")
    channels, tokens = queries.shape
    depth = out_grad.shape[1]
    width = channels // ctx_size
    order = residues.shape[0]
    columns = halves(width)
    count = order // 8
    blocks = tokens // STEP
    f32, bf16 = jnp.float32, jnp.bfloat16
    offset = pl.multiple_of(me * width, width) if residues.shape[1] != width else 0

    def links(kind, outgoing, incoming):
        return (outgoing, incoming, sends.at[kind], arrivals.at[kind])

    product_links = links(0, product_out, product_in)
    conv_out_links = links(1, conv_out_out, conv_out_in)
    conv_grad_links = links(2, conv_grad_out, conv_grad_in)
    product_grad_links = links(3, product_grad_out, product_grad_in)

    def send_or_keep(link, other):
        @pl.when(other != me)
        def _():
            exchange(*link, me, other).start()

        @pl.when(other == me)
        def _():
            link[1][me] = link[0][me]

    def await_slot(link, other):
        @pl.when(other != me)
        def _():
            expect(*link, other).wait_recv()

    def weight_copy(shard):
        return pltpu.make_async_copy(
            out_weight.at[:, pl.ds(pl.multiple_of(shard * depth, depth), depth)],
            weight.at[shard],
            weight_sems.at[shard],
        )

    def shard_copy(source, shard, going_up):
        return pltpu.make_async_remote_copy(
            src_ref=source,
            dst_ref=gathered.at[shard],
            send_sem=(up_sends if going_up else down_sends).at[shard],
            recv_sem=shard_arrivals.at[shard],
            device_id=axis_device("chan", place + 1 if going_up else place - 1),
            device_id_type=pl.DeviceIdType.MESH,
        )

    weight_copy(place).start()
    for distance in range(1, chan_size):
        for shard, present in (
            (place - distance, place >= distance),
            (place + distance, place + distance < chan_size),
        ):

            @pl.when(present)
            def _():
                weight_copy(shard).start()

    barrier = pltpu.get_barrier_semaphore()
    for step in range(1, ctx_size):
        pl.semaphore_signal(
            barrier,
            inc=1,
            device_id=axis_device("ctx", lax.rem(me + step, ctx_size)),
            device_id_type=pl.DeviceIdType.MESH,
        )
    for step in range(1, chan_size):
        pl.semaphore_signal(
            barrier,
            inc=1,
            device_id=axis_device("chan", lax.rem(place + step, chan_size)),
            device_id_type=pl.DeviceIdType.MESH,
        )
    pl.semaphore_wait(barrier, ctx_size + chan_size - 2)

    @pl.when(place < chan_size - 1)
    def _():
        shard_copy(out_grad, place, True).start()

    @pl.when(place > 0)
    def _():
        shard_copy(out_grad, place, False).start()

    @pl.loop(0, ctx_size)
    def _(step):
        other = lax.rem(me + 1 + step, ctx_size)
        rows = pl.ds(pl.multiple_of(other * width, width), width)
        pair = keys[rows, :].astype(f32) * values[rows, :].astype(f32)
        product_out[other] = pair.astype(bf16).astype(f32).T.astype(bf16)
        send_or_keep(product_links, other)

    tile = min(channels, 512)

    def multiply(source, shard, first):
        @pl.loop(0, channels // tile)
        def _(index):
            rows = pl.ds(pl.multiple_of(index * tile, tile), tile)
            term = lax.dot_general(
                weight[shard, rows, :],
                source[...],
                (((1,), (1,)), ((), ())),
                preferred_element_type=f32,
            )
            mixer[rows, :] = term if first else mixer[rows, :] + term

    weight_copy(place).wait()
    multiply(out_grad, place, True)

    def gather_step(distance):
        sides = (
            (place - distance, place >= distance, place < chan_size - 1, True),
            (place + distance, place + distance < chan_size, place > 0, False),
        )
        for shard, present, onward, going_up in sides:

            @pl.when(present)
            def _():
                shard_copy(gathered.at[shard], shard, going_up).wait_recv()

                @pl.when(onward)
                def _():
                    shard_copy(gathered.at[shard], shard, going_up).start()

        for shard, present, onward, going_up in sides:

            @pl.when(present)
            def _():
                weight_copy(shard).wait()
                multiply(gathered.at[shard], shard, False)

    def mode_groups(start, lanes):
        groups = []
        for g in range(count):
            where = (pl.ds(8 * g, 8), pl.ds(offset + start, lanes))
            rate = decay_rates[where]
            groups.append((jnp.exp(-rate), residues[where] * jnp.sqrt(2.0 * rate)))
        return groups

    def causal_scan():
        modes = [mode_groups(*column) for column in columns]

        def chunk(slot, state):
            await_slot(product_links, slot)

            def block(index, state):
                base = pl.multiple_of(index * STEP, STEP)
                state = [list(group) for group in state]
                for position, (start, lanes) in enumerate(columns):
                    where = (slot, pl.ds(base, STEP), pl.ds(start, lanes))
                    rows = product_in[where].astype(f32)
                    totals = []
                    for step in range(STEP):
                        row = jnp.broadcast_to(rows[step : step + 1, :], (8, lanes))
                        total = None
                        for g in range(count):
                            decay, gain = modes[position][g]
                            held = decay * state[position][g] + row
                            state[position][g] = held
                            total = gain * held if total is None else total + gain * held
                        totals.append(total)
                    conv_out_out[where] = jnp.concatenate(
                        [fold_rows(totals[:8]), fold_rows(totals[8:])], axis=0
                    ).astype(bf16)
                return tuple(tuple(group) for group in state)

            state = lax.fori_loop(0, blocks, block, state)
            send_or_keep(conv_out_links, slot)
            return state

        zero = tuple(
            tuple(jnp.zeros((8, lanes), f32) for _ in range(count)) for _, lanes in columns
        )
        lax.fori_loop(0, ctx_size, chunk, zero)

    def reverse_scan():
        modes = [mode_groups(*column) for column in columns]

        def chunk(step_index, state):
            slot = ctx_size - 1 - step_index
            await_slot(conv_grad_links, slot)

            def block(index, state):
                base = pl.multiple_of((blocks - 1 - index) * STEP, STEP)
                state = [[list(item) for item in group] for group in state]
                for position, (start, lanes) in enumerate(columns):
                    where = (slot, pl.ds(base, STEP), pl.ds(start, lanes))
                    source = product_in[where].astype(f32)
                    drive = conv_grad_in[where].astype(f32)
                    totals = [None] * STEP
                    for step in reversed(range(STEP)):
                        source_row = jnp.broadcast_to(source[step : step + 1, :], (8, lanes))
                        drive_row = jnp.broadcast_to(drive[step : step + 1, :], (8, lanes))
                        total = None
                        for g in range(count):
                            decay, gain = modes[position][g]
                            held, moment, plain_sum, moment_sum = state[position][g]
                            moment = decay * (moment + held)
                            held = decay * held + drive_row
                            state[position][g] = [
                                held,
                                moment,
                                plain_sum + source_row * held,
                                moment_sum + source_row * moment,
                            ]
                            total = gain * held if total is None else total + gain * held
                        totals[step] = total
                    product_grad_out[where] = jnp.concatenate(
                        [fold_rows(totals[:8]), fold_rows(totals[8:])], axis=0
                    ).astype(bf16)
                return tuple(tuple(tuple(item) for item in group) for group in state)

            state = lax.fori_loop(0, blocks, block, state)
            send_or_keep(product_grad_links, slot)
            return state

        zero = tuple(
            tuple((jnp.zeros((8, lanes), f32),) * 4 for _ in range(count)) for _, lanes in columns
        )
        final = lax.fori_loop(0, ctx_size, chunk, zero)
        for position, (start, lanes) in enumerate(columns):
            for g in range(count):
                where = (pl.ds(8 * g, 8), pl.ds(offset + start, lanes))
                rate, amplitude = decay_rates[where], residues[where]
                root = jnp.sqrt(2.0 * rate)
                plain_sum, moment_sum = final[position][g][2:]
                put = (pl.ds(8 * g, 8), pl.ds(start, lanes))
                resid_grad[put] = root * plain_sum
                decay_grad[put] = amplitude * root * (0.5 * plain_sum - rate * moment_sum)

    for distance in range(1, chan_size):
        gather_step(distance)
        if distance == 1:
            causal_scan()
    if chan_size == 1:
        causal_scan()

    @pl.loop(0, ctx_size)
    def _(step):
        other = lax.rem(me + 1 + step, ctx_size)
        rows = pl.ds(pl.multiple_of(other * width, width), width)
        pair = mixer[rows, :].astype(bf16).astype(f32) * queries[rows, :].astype(f32)
        conv_grad_out[other] = pair.astype(bf16).astype(f32).T.astype(bf16)
        send_or_keep(conv_grad_links, other)

    reverse_scan()

    @pl.loop(0, ctx_size)
    def _(slot):
        await_slot(conv_out_links, slot)
        rows = pl.ds(pl.multiple_of(slot * width, width), width)
        result = conv_out_in[slot].astype(f32).T
        query_grad[rows, :] = (mixer[rows, :].astype(bf16).astype(f32) * result).astype(bf16)

    @pl.loop(0, ctx_size)
    def _(slot):
        await_slot(product_grad_links, slot)
        rows = pl.ds(pl.multiple_of(slot * width, width), width)
        result = product_grad_in[slot].astype(f32).T
        key_grad[rows, :] = (result * values[rows, :].astype(f32)).astype(bf16)
        value_grad[rows, :] = (result * keys[rows, :].astype(f32)).astype(bf16)

    @pl.loop(0, ctx_size)
    def _(other):
        @pl.when(other != me)
        def _():
            for link in (product_links, conv_out_links, conv_grad_links, product_grad_links):
                exchange(*link, me, other).wait_send()

    for distance in range(chan_size):
        for shard, present, onward, going_up in (
            (place - distance, place >= distance, place < chan_size - 1, True),
            (place + distance, place + distance < chan_size, place > 0, False),
        ):

            @pl.when(present & onward)
            def _():
                source = out_grad if distance == 0 else gathered.at[shard]
                shard_copy(source, shard, going_up).wait_send()


def local(queries, keys, values, out_grad, out_weight, residues, decay_rates):
    channels, tokens = queries.shape
    chan_size = lax.axis_size("chan")
    ctx_size = lax.axis_size("ctx")
    width = channels // ctx_size
    depth = out_grad.shape[1]
    order = residues.shape[0]
    if width % 128:
        offset = lax.axis_index("ctx") * width
        residues = lax.dynamic_slice_in_dim(residues, offset, width, 1)
        decay_rates = lax.dynamic_slice_in_dim(decay_rates, offset, width, 1)
    gate = jax.ShapeDtypeStruct((channels, tokens), jnp.bfloat16)
    grads = jax.ShapeDtypeStruct((order, width), jnp.float32)
    vmem = pl.BlockSpec(memory_space=pltpu.VMEM)
    slots = pltpu.VMEM((ctx_size, tokens, width), jnp.bfloat16)
    dma = pltpu.SemaphoreType.DMA
    return tuple(
        pl.pallas_call(
            functools.partial(body, chan_size, ctx_size),
            out_shape=(gate, gate, gate, grads, grads),
            in_specs=[vmem, vmem, vmem, vmem, pl.BlockSpec(memory_space=pl.ANY), vmem, vmem],
            out_specs=(vmem,) * 5,
            scratch_shapes=[
                pltpu.VMEM((chan_size, channels, depth), jnp.bfloat16),
                pltpu.VMEM((chan_size, tokens, depth), jnp.bfloat16),
                pltpu.VMEM((channels, tokens), jnp.float32),
                *[slots] * 8,
                dma((chan_size,)),
                dma((chan_size,)),
                dma((chan_size,)),
                dma((chan_size,)),
                dma((4, ctx_size)),
                dma((4, ctx_size)),
            ],
            compiler_params=pltpu.CompilerParams(
                collective_id=0, has_side_effects=True, vmem_limit_bytes=56 * 1024 * 1024
            ),
        )(queries, keys, values, out_grad, out_weight, residues, decay_rates)
    )


def solution(mesh):
    placed = (
        P("chan", "ctx"),
        P("chan", "ctx"),
        P("chan", "ctx"),
        P("ctx", "chan"),
        P("chan", None),
        P(None, "chan"),
        P(None, "chan"),
    )
    return jax.shard_map(
        local,
        mesh=mesh,
        in_specs=placed,
        out_specs=(
            P("chan", "ctx"),
            P("chan", "ctx"),
            P("chan", "ctx"),
            P(None, ("chan", "ctx")),
            P(None, ("chan", "ctx")),
        ),
        check_vma=False,
    )
```

```python
import functools

import jax
import jax.numpy as jnp
from jax import lax
from jax.experimental import pallas as pl
from jax.experimental.pallas import tpu as pltpu
from jax.sharding import PartitionSpec as P

STEP = 16
PIECES = 4


def halves(width):
    lanes = min(width, 128)
    return [(start, lanes) for start in range(0, width, lanes)]


def fold_rows(rows):
    lanes = rows[0].shape[1]
    sub = lax.broadcasted_iota(jnp.int32, (8, lanes), 0)
    low4, low2, low1 = sub < 4, (sub & 2) == 0, (sub & 1) == 0
    four = []
    for i in range(4):
        a, b = rows[i], rows[i + 4]
        four.append(jnp.where(low4, a, b) + pltpu.roll(jnp.where(low4, b, a), 4, 0))
    two = []
    for i in range(2):
        a, b = four[i], four[i + 2]
        two.append(
            jnp.where(low2, a, pltpu.roll(b, 2, 0)) + jnp.where(low2, pltpu.roll(a, 6, 0), b)
        )
    a, b = two
    return jnp.where(low1, a, pltpu.roll(b, 1, 0)) + jnp.where(low1, pltpu.roll(a, 7, 0), b)


def elementwise(left, right):
    return (left.astype(jnp.float32) * right.astype(jnp.float32)).astype(jnp.bfloat16)


def axis_device(axis, index):
    return {axis: index}


def exchange(outgoing, incoming, sends, arrivals, me, other):
    return pltpu.make_async_remote_copy(
        src_ref=outgoing.at[other],
        dst_ref=incoming.at[me],
        send_sem=sends.at[other],
        recv_sem=arrivals.at[me],
        device_id=axis_device("ctx", other),
        device_id_type=pl.DeviceIdType.MESH,
    )


def expect(outgoing, incoming, sends, arrivals, other):
    return pltpu.make_async_remote_copy(
        src_ref=outgoing.at[other],
        dst_ref=incoming.at[other],
        send_sem=sends.at[other],
        recv_sem=arrivals.at[other],
        device_id=axis_device("ctx", other),
        device_id_type=pl.DeviceIdType.MESH,
    )


def body(
    chan_size,
    ctx_size,
    queries,
    keys,
    values,
    out_grad,
    out_weight,
    residues,
    decay_rates,
    mixer_out,
    conv_out,
    product_grad,
    plain_out,
    plain_scale,
    slope_out,
    slope_scale,
    weight,
    gathered,
    mixer,
    product_out,
    product_in,
    conv_out_out,
    conv_out_in,
    conv_grad_out,
    conv_grad_in,
    product_grad_out,
    product_grad_in,
    weight_sems,
    shard_arrivals,
    up_sends,
    down_sends,
    sends,
    arrivals,
):
    place = lax.axis_index("chan")
    me = lax.axis_index("ctx")
    channels, tokens = queries.shape
    depth = out_grad.shape[1]
    piece = depth // PIECES
    width = channels // ctx_size
    order = residues.shape[0]
    columns = halves(width)
    count = order // 8
    blocks = tokens // STEP
    f32, bf16 = jnp.float32, jnp.bfloat16
    offset = pl.multiple_of(me * width, width) if residues.shape[1] != width else 0

    def links(kind, outgoing, incoming):
        return (outgoing, incoming, sends.at[kind], arrivals.at[kind])

    product_links = links(0, product_out, product_in)
    conv_out_links = links(1, conv_out_out, conv_out_in)
    conv_grad_links = links(2, conv_grad_out, conv_grad_in)
    product_grad_links = links(3, product_grad_out, product_grad_in)

    def send_or_keep(link, other):
        @pl.when(other != me)
        def _():
            exchange(*link, me, other).start()

        @pl.when(other == me)
        def _():
            link[1][me] = link[0][me]

    def await_slot(link, other):
        @pl.when(other != me)
        def _():
            expect(*link, other).wait_recv()

    def weight_copy(shard):
        return pltpu.make_async_copy(
            out_weight.at[:, pl.ds(pl.multiple_of(shard * depth, depth), depth)],
            weight.at[shard],
            weight_sems.at[shard],
        )

    def shard_copy(shard, part, going_up, own=False):
        return pltpu.make_async_remote_copy(
            src_ref=out_grad.at[:, pl.ds(part * piece, piece)] if own else gathered.at[shard, part],
            dst_ref=gathered.at[shard, part],
            send_sem=(up_sends if going_up else down_sends).at[shard, part],
            recv_sem=shard_arrivals.at[shard, part],
            device_id=axis_device("chan", place + 1 if going_up else place - 1),
            device_id_type=pl.DeviceIdType.MESH,
        )

    weight_copy(place).start()
    for distance in range(1, chan_size):
        for shard, present in (
            (place - distance, place >= distance),
            (place + distance, place + distance < chan_size),
        ):

            @pl.when(present)
            def _():
                weight_copy(shard).start()

    barrier = pltpu.get_barrier_semaphore()
    for step in range(1, ctx_size):
        pl.semaphore_signal(
            barrier,
            inc=1,
            device_id=axis_device("ctx", lax.rem(me + step, ctx_size)),
            device_id_type=pl.DeviceIdType.MESH,
        )
    for step in range(1, chan_size):
        pl.semaphore_signal(
            barrier,
            inc=1,
            device_id=axis_device("chan", lax.rem(place + step, chan_size)),
            device_id_type=pl.DeviceIdType.MESH,
        )
    pl.semaphore_wait(barrier, ctx_size + chan_size - 2)

    for part in range(PIECES):

        @pl.when(place < chan_size - 1)
        def _():
            shard_copy(place, part, True, True).start()

        @pl.when(place > 0)
        def _():
            shard_copy(place, part, False, True).start()

    @pl.loop(0, ctx_size)
    def _(step):
        other = lax.rem(me + 1 + step, ctx_size)
        rows = pl.ds(pl.multiple_of(other * width, width), width)
        pair = keys[rows, :].astype(f32) * values[rows, :].astype(f32)
        product_out[other] = pair.astype(bf16).astype(f32).T.astype(bf16)
        send_or_keep(product_links, other)

    tile = min(channels, 512)

    def multiply(source, shard, taken, first):
        @pl.loop(0, channels // tile)
        def _(index):
            rows = pl.ds(pl.multiple_of(index * tile, tile), tile)
            term = lax.dot_general(
                weight[shard, rows, taken],
                source[...],
                (((1,), (1,)), ((), ())),
                preferred_element_type=f32,
            )
            mixer[rows, :] = term if first else mixer[rows, :] + term

    weight_copy(place).wait()
    multiply(out_grad, place, slice(None), True)

    def gather_step(distance):
        sides = (
            (place - distance, place >= distance, place < chan_size - 1, True),
            (place + distance, place + distance < chan_size, place > 0, False),
        )
        for part in range(PIECES):
            for shard, present, onward, going_up in sides:

                @pl.when(present)
                def _():
                    shard_copy(shard, part, going_up).wait_recv()

                    @pl.when(onward)
                    def _():
                        shard_copy(shard, part, going_up).start()

            for shard, present, onward, going_up in sides:

                @pl.when(present)
                def _():
                    if part == 0:
                        weight_copy(shard).wait()
                    taken = pl.ds(part * piece, piece)
                    multiply(gathered.at[shard, part], shard, taken, False)

    def mode_groups(start, lanes):
        groups = []
        for g in range(count):
            where = (pl.ds(8 * g, 8), pl.ds(offset + start, lanes))
            rate = decay_rates[where]
            groups.append((jnp.exp(-rate), residues[where] * jnp.sqrt(2.0 * rate)))
        return groups

    def causal_scan():
        modes = [mode_groups(*column) for column in columns]

        def chunk(slot, state):
            await_slot(product_links, slot)

            def block(index, state):
                base = pl.multiple_of(index * STEP, STEP)
                state = [list(group) for group in state]
                for position, (start, lanes) in enumerate(columns):
                    where = (slot, pl.ds(base, STEP), pl.ds(start, lanes))
                    rows = product_in[where].astype(f32)
                    totals = []
                    for step in range(STEP):
                        row = jnp.broadcast_to(rows[step : step + 1, :], (8, lanes))
                        total = None
                        for g in range(count):
                            decay, gain = modes[position][g]
                            held = decay * state[position][g] + row
                            state[position][g] = held
                            total = gain * held if total is None else total + gain * held
                        totals.append(total)
                    conv_out_out[where] = jnp.concatenate(
                        [fold_rows(totals[:8]), fold_rows(totals[8:])], axis=0
                    ).astype(bf16)
                return tuple(tuple(group) for group in state)

            state = lax.fori_loop(0, blocks, block, state)
            send_or_keep(conv_out_links, slot)
            return state

        zero = tuple(
            tuple(jnp.zeros((8, lanes), f32) for _ in range(count)) for _, lanes in columns
        )
        lax.fori_loop(0, ctx_size, chunk, zero)

    def reverse_scan():
        modes = [mode_groups(*column) for column in columns]

        def chunk(step_index, state):
            slot = ctx_size - 1 - step_index
            await_slot(conv_grad_links, slot)

            def block(index, state):
                base = pl.multiple_of((blocks - 1 - index) * STEP, STEP)
                state = [[list(item) for item in group] for group in state]
                for position, (start, lanes) in enumerate(columns):
                    where = (slot, pl.ds(base, STEP), pl.ds(start, lanes))
                    source = product_in[where].astype(f32)
                    drive = conv_grad_in[where].astype(f32)
                    totals = [None] * STEP
                    for step in reversed(range(STEP)):
                        source_row = jnp.broadcast_to(source[step : step + 1, :], (8, lanes))
                        drive_row = jnp.broadcast_to(drive[step : step + 1, :], (8, lanes))
                        total = None
                        for g in range(count):
                            decay, gain = modes[position][g]
                            held, moment, plain_sum, moment_sum = state[position][g]
                            moment = decay * (moment + held)
                            held = decay * held + drive_row
                            state[position][g] = [
                                held,
                                moment,
                                plain_sum + source_row * held,
                                moment_sum + source_row * moment,
                            ]
                            total = gain * held if total is None else total + gain * held
                        totals[step] = total
                    product_grad_out[where] = jnp.concatenate(
                        [fold_rows(totals[:8]), fold_rows(totals[8:])], axis=0
                    ).astype(bf16)
                return tuple(tuple(tuple(item) for item in group) for group in state)

            state = lax.fori_loop(0, blocks, block, state)
            send_or_keep(product_grad_links, slot)
            return state

        zero = tuple(
            tuple((jnp.zeros((8, lanes), f32),) * 4 for _ in range(count)) for _, lanes in columns
        )
        final = lax.fori_loop(0, ctx_size, chunk, zero)
        for position, (start, lanes) in enumerate(columns):
            for g in range(count):
                where = (pl.ds(8 * g, 8), pl.ds(offset + start, lanes))
                rate, amplitude = decay_rates[where], residues[where]
                root = jnp.sqrt(2.0 * rate)
                plain_sum, moment_sum = final[position][g][2:]
                put = (pl.ds(8 * g, 8), pl.ds(start, lanes))
                plain_out[put] = plain_sum
                plain_scale[put] = root
                slope_out[put] = 0.5 * plain_sum - rate * moment_sum
                slope_scale[put] = amplitude * root

    for distance in range(1, chan_size):
        gather_step(distance)
        if distance == 1:
            causal_scan()
    if chan_size == 1:
        causal_scan()

    @pl.loop(0, ctx_size)
    def _(step):
        other = lax.rem(me + 1 + step, ctx_size)
        rows = pl.ds(pl.multiple_of(other * width, width), width)
        rounded = mixer[rows, :].astype(bf16)
        mixer_out[rows, :] = rounded
        pair = rounded.astype(f32) * queries[rows, :].astype(f32)
        conv_grad_out[other] = pair.astype(bf16).astype(f32).T.astype(bf16)
        send_or_keep(conv_grad_links, other)

    reverse_scan()

    @pl.loop(0, ctx_size)
    def _(slot):
        await_slot(conv_out_links, slot)
        rows = pl.ds(pl.multiple_of(slot * width, width), width)
        conv_out[rows, :] = conv_out_in[slot].astype(f32).T.astype(bf16)

    @pl.loop(0, ctx_size)
    def _(slot):
        await_slot(product_grad_links, slot)
        rows = pl.ds(pl.multiple_of(slot * width, width), width)
        product_grad[rows, :] = product_grad_in[slot].astype(f32).T.astype(bf16)

    @pl.loop(0, ctx_size)
    def _(other):
        @pl.when(other != me)
        def _():
            for link in (product_links, conv_out_links, conv_grad_links, product_grad_links):
                exchange(*link, me, other).wait_send()

    for distance in range(chan_size):
        for shard, present, onward, going_up in (
            (place - distance, place >= distance, place < chan_size - 1, True),
            (place + distance, place + distance < chan_size, place > 0, False),
        ):

            @pl.when(present & onward)
            def _():
                for part in range(PIECES):
                    shard_copy(shard, part, going_up, distance == 0).wait_send()


def local(queries, keys, values, out_grad, out_weight, residues, decay_rates):
    channels, tokens = queries.shape
    chan_size = lax.axis_size("chan")
    ctx_size = lax.axis_size("ctx")
    width = channels // ctx_size
    depth = out_grad.shape[1]
    order = residues.shape[0]
    if width % 128:
        offset = lax.axis_index("ctx") * width
        residues = lax.dynamic_slice_in_dim(residues, offset, width, 1)
        decay_rates = lax.dynamic_slice_in_dim(decay_rates, offset, width, 1)
    gate = jax.ShapeDtypeStruct((channels, tokens), jnp.bfloat16)
    grads = jax.ShapeDtypeStruct((order, width), jnp.float32)
    vmem = pl.BlockSpec(memory_space=pltpu.VMEM)
    slots = pltpu.VMEM((ctx_size, tokens, width), jnp.bfloat16)
    dma = pltpu.SemaphoreType.DMA
    mixer, conv_out, product_grad, plain, plain_scale, slope, slope_scale = pl.pallas_call(
            functools.partial(body, chan_size, ctx_size),
            out_shape=(gate,) * 3 + (grads,) * 4,
            in_specs=[vmem, vmem, vmem, vmem, pl.BlockSpec(memory_space=pl.ANY), vmem, vmem],
            out_specs=(vmem,) * 7,
            scratch_shapes=[
                pltpu.VMEM((chan_size, channels, depth), jnp.bfloat16),
                pltpu.VMEM((chan_size, PIECES, tokens, depth // PIECES), jnp.bfloat16),
                pltpu.VMEM((channels, tokens), jnp.float32),
                *[slots] * 8,
                dma((chan_size,)),
                dma((chan_size, PIECES)),
                dma((chan_size, PIECES)),
                dma((chan_size, PIECES)),
                dma((4, ctx_size)),
                dma((4, ctx_size)),
            ],
            compiler_params=pltpu.CompilerParams(
                collective_id=0, has_side_effects=True, vmem_limit_bytes=56 * 1024 * 1024
            ),
    )(queries, keys, values, out_grad, out_weight, residues, decay_rates)
    return (
        elementwise(mixer, conv_out),
        elementwise(product_grad, values),
        elementwise(product_grad, keys),
        plain_scale * plain,
        slope_scale * slope,
    )


def solution(mesh):
    placed = (
        P("chan", "ctx"),
        P("chan", "ctx"),
        P("chan", "ctx"),
        P("ctx", "chan"),
        P("chan", None),
        P(None, "chan"),
        P(None, "chan"),
    )
    return jax.shard_map(
        local,
        mesh=mesh,
        in_specs=placed,
        out_specs=(
            P("chan", "ctx"),
            P("chan", "ctx"),
            P("chan", "ctx"),
            P(None, ("chan", "ctx")),
            P(None, ("chan", "ctx")),
        ),
        check_vma=False,
    )
```
